32 devices in a mesh: head: 4 (over y, x), ctx: 8 (over z, core).
Axes of the slice: x: 2, y: 2, z: 4, core: 2. Of those that a mesh axis runs over, the one named last changes fastest.
Arguments:
- query_in: bfloat16 [4096, 4096], P(('ctx', 'head')), may hold values from -6 to 6
- key_in: bfloat16 [4096, 1024], P(('ctx', 'head')), may hold values from -6 to 6
- value_in: bfloat16 [4096, 1024], P(('ctx', 'head')), may hold values from -6 to 6
- attn_out: bfloat16 [4096, 4096], P(('ctx', 'head')), may hold values from -2 to 2
- out_grad: bfloat16 [4096, 4096], P(('ctx', 'head')), may hold values from -6 to 6
- log_norm: float32 [4096, 32], P(('ctx', 'head')), may hold values from 4 to 8
- doc_ids: int32 [4096], replicated, may hold values from 0 to 15, never falling along the last dimension, each value on 1 to 512 neighbouring positions
Outputs:
- query_grad: bfloat16 [4096, 4096], P(('ctx', 'head'))
- key_grad: bfloat16 [4096, 1024], P(('ctx', 'head'))
- value_grad: bfloat16 [4096, 1024], P(('ctx', 'head'))
The draws below stay inside these ranges and needn't reach their ends.
Inputs may be any that keep to these rules, and one draw needn't show every extreme that they name: `doc_ids`: document numbers never fall along the sequence and start at 0; every document has 1 to 512 tokens and one has exactly 512.
All inputs are finite; a program needn't handle non-finite values.
Results may differ from the reference program's by a relative error of at most 0.0049.
Values may be sent and summed in bfloat16 or wider, within the bound.
No kernel may reach another device: no remote copies, remote signals or barrier semaphores. Data moves between devices by JAX's collectives and lax.ppermute only.
A program may use at most 128 MiB of HBM per device.

```python
import math
import jax
import jax.numpy as jnp
import numpy as np
from jax import lax

HEADS = 32
KV_HEADS = 8
HEAD_DIM = 128
SEQ = 4096
DOC_MOST = 512
DOCS = 16


def block_levels(own_key, dims, cuts, low, largest):
    def one(axis_at, blocks):
        steps = jax.random.uniform(jax.random.fold_in(jax.random.fold_in(own_key, 6), axis_at), (blocks,), jnp.float32, low / len(cuts), largest / len(cuts))
        return jnp.repeat(jnp.exp(steps), dims[axis_at] // blocks).reshape((-1,) + (1,) * (len(dims) - axis_at - 1))

    gain = one(*cuts[0])
    for cut in cuts[1:]:
        gain = gain * one(*cut)
    return gain


def length_profile(count, total, most, lean):
    portions = [(1 << 20) // math.isqrt(grade ** lean) + 1 for grade in range(2, count + 1)]
    surplus, holding = total - most - (count - 1), [1] * (count - 1)
    while surplus > 0:
        movable = [i for i in range(count - 1) if holding[i] < most]
        pool, remaining = sum([portions[i] for i in movable]), surplus
        for i in movable:
            more = min(most - holding[i], max(1, remaining * portions[i] // pool), surplus)
            holding[i] = holding[i] + more
            surplus = surplus - more
    return np.array([most] + holding)


def uneven_parts(own_key, amount, total, limit, lean):
    if amount == 2:
        one = jax.random.randint(own_key, (), max(1, total - limit), min(limit, total - 1) + 1)
        return jnp.stack([one, total - one])
    sizes = jnp.asarray(length_profile(amount, total, limit, lean), jnp.int32)
    pairs = (amount - 1) // 2
    source_of, taker = sizes[1:1 + 2 * pairs:2], sizes[2:2 + 2 * pairs:2]
    slack = jnp.minimum(source_of - 1, limit - taker)
    moved = jax.random.randint(jax.random.fold_in(own_key, 1), (pairs,), 0, 1 << 20) % (slack + 1)
    sizes = sizes.at[1:1 + 2 * pairs:2].set(source_of - moved).at[2:2 + 2 * pairs:2].set(taker + moved)
    return sizes[jax.random.permutation(jax.random.fold_in(own_key, 2), amount)]


def centred(own_key, dims, deviation, reach, pieces=(), kind=jnp.bfloat16):
    drawn = deviation * jax.random.normal(own_key, dims, jnp.float32)
    if pieces:
        drawn = drawn * block_levels(own_key, dims, pieces, -0.22, 0.18)
    return jnp.clip(drawn, -reach, reach).astype(kind)


def setup_inputs(seed: int = 0) -> dict:
    splits = jax.random.split(jax.random.key(seed), 8)
    query_in = centred(splits[0], (SEQ, HEADS * HEAD_DIM), 1.0, 6.0, ((0, 32),))
    key_in = centred(splits[1], (SEQ, KV_HEADS * HEAD_DIM), 1.0, 6.0, ((0, 32),))
    value_in = centred(splits[2], (SEQ, KV_HEADS * HEAD_DIM), 1.0, 6.0, ((0, 32),))
    attn_out = centred(splits[3], (SEQ, HEADS * HEAD_DIM), 0.3, 2.0, ((0, 32),))
    out_grad = centred(splits[4], (SEQ, HEADS * HEAD_DIM), 1.0, 6.0, ((0, 32),))
    log_norm = jnp.clip(4.0 + 4.0 * jax.random.uniform(splits[5], (SEQ, HEADS), jnp.float32) ** block_levels(splits[5], (SEQ, HEADS), ((0, 32),), -0.2, 0.2), 4.0, 8.0)
    doc_ids = jnp.searchsorted(jnp.cumsum(uneven_parts(splits[6], DOCS, SEQ, DOC_MOST, 0)), jnp.arange(SEQ), side="right").astype(jnp.int32)
    return {"query_in": query_in, "key_in": key_in, "value_in": value_in, "attn_out": attn_out, "out_grad": out_grad, "log_norm": log_norm, "doc_ids": doc_ids}


def lower_round(values):
    return lax.optimization_barrier(values.astype(jnp.bfloat16)).astype(jnp.float32)


def block_terms(query_rows, dout_rows, norm_rows, delta_rows, query_ids, query_start, key_rows, value_rows, key_ids, key_start):
    r = query_rows.shape[0]
    c = key_rows.shape[0]
    kv_local = key_rows.shape[1] // HEAD_DIM
    heads_local = query_rows.shape[1] // HEAD_DIM
    group = heads_local // kv_local
    scaling = HEAD_DIM ** -0.5
    query_heads = query_rows.astype(jnp.float32).reshape(r, kv_local, group, HEAD_DIM)
    dout_heads = dout_rows.astype(jnp.float32).reshape(r, kv_local, group, HEAD_DIM)
    key_heads = key_rows.astype(jnp.float32).reshape(c, kv_local, HEAD_DIM)
    value_heads = value_rows.astype(jnp.float32).reshape(c, kv_local, HEAD_DIM)
    highest = lax.Precision.HIGHEST
    scores = jnp.einsum("qgjd,kgd->gjqk", query_heads, key_heads, precision=highest) * scaling
    norm_cols = jnp.transpose(norm_rows.reshape(r, kv_local, group), (1, 2, 0))[..., None]
    delta_cols = jnp.transpose(delta_rows.reshape(r, kv_local, group), (1, 2, 0))[..., None]
    query_pos = query_start + jnp.arange(r, dtype=jnp.int32)
    key_pos = key_start + jnp.arange(c, dtype=jnp.int32)
    allowed = (query_ids[:, None] == key_ids[None, :]) & (query_pos[:, None] >= key_pos[None, :])
    weights = jnp.where(allowed, jnp.exp(scores - norm_cols), 0.0)
    weights_low = lower_round(weights)
    grad_value = jnp.einsum("gjqk,qgjd->kgd", weights_low, dout_heads, precision=highest)
    prob_grad = jnp.einsum("qgjd,kgd->gjqk", dout_heads, value_heads, precision=highest)
    score_grad = lower_round(weights * (prob_grad - delta_cols))
    grad_query = jnp.einsum("gjqk,kgd->qgjd", score_grad, key_heads, precision=highest) * scaling
    grad_key = jnp.einsum("gjqk,qgjd->kgd", score_grad, query_heads, precision=highest) * scaling
    return (grad_query.reshape(r, heads_local * HEAD_DIM), grad_key.reshape(c, kv_local * HEAD_DIM),
            grad_value.reshape(c, kv_local * HEAD_DIM))


def reference(query_in, key_in, value_in, attn_out, out_grad, log_norm, doc_ids):
    seq_len = query_in.shape[0]
    block_len = math.gcd(seq_len, 256)
    block_count = seq_len // block_len
    head_count = query_in.shape[1] // HEAD_DIM
    product = out_grad.astype(jnp.float32) * attn_out.astype(jnp.float32)
    delta_all = jnp.sum(product.reshape(seq_len, head_count, HEAD_DIM), axis=2)
    kv_width = key_in.shape[1]

    def query_step(carry, index):
        key_total, value_total = carry
        query_start = index * block_len
        query_rows = lax.dynamic_slice_in_dim(query_in, query_start, block_len, 0)
        dout_rows = lax.dynamic_slice_in_dim(out_grad, query_start, block_len, 0)
        norm_rows = lax.dynamic_slice_in_dim(log_norm, query_start, block_len, 0)
        delta_rows = lax.dynamic_slice_in_dim(delta_all, query_start, block_len, 0)
        query_ids = lax.dynamic_slice_in_dim(doc_ids, query_start, block_len, 0)
        first_doc = query_ids[0]
        doc_begin = jnp.sum((doc_ids < first_doc).astype(jnp.int32)).astype(jnp.int32)
        lowest = (doc_begin // block_len).astype(jnp.int32)

        def key_step(other, inner):
            query_acc, key_acc, value_acc = inner
            key_start = other * block_len
            key_rows = lax.dynamic_slice_in_dim(key_in, key_start, block_len, 0)
            value_rows = lax.dynamic_slice_in_dim(value_in, key_start, block_len, 0)
            key_ids = lax.dynamic_slice_in_dim(doc_ids, key_start, block_len, 0)
            grad_query, grad_key, grad_value = block_terms(query_rows, dout_rows, norm_rows, delta_rows, query_ids,
                                                           query_start, key_rows, value_rows, key_ids, key_start)
            old_key = lax.dynamic_slice_in_dim(key_acc, key_start, block_len, 0)
            old_value = lax.dynamic_slice_in_dim(value_acc, key_start, block_len, 0)
            key_acc = lax.dynamic_update_slice_in_dim(key_acc, old_key + grad_key, key_start, 0)
            value_acc = lax.dynamic_update_slice_in_dim(value_acc, old_value + grad_value, key_start, 0)
            return query_acc + grad_query, key_acc, value_acc

        start_acc = jnp.zeros((block_len, query_in.shape[1]), jnp.float32)
        query_acc, key_total, value_total = lax.fori_loop(lowest, index + 1, key_step,
                                                          (start_acc, key_total, value_total))
        return (key_total, value_total), query_acc.astype(jnp.bfloat16)

    start = (jnp.zeros((seq_len, kv_width), jnp.float32), jnp.zeros((seq_len, kv_width), jnp.float32))
    (key_total, value_total), query_blocks = lax.scan(query_step, start,
                                                      jnp.arange(block_count, dtype=jnp.int32))
    query_grad = query_blocks.reshape(seq_len, query_in.shape[1])
    return query_grad, key_total.astype(jnp.bfloat16), value_total.astype(jnp.bfloat16)
```

```python
import functools

import jax
import jax.numpy as jnp
from jax import lax
from jax.experimental import pallas as pl
from jax.experimental.pallas import tpu as pltpu
from jax.sharding import PartitionSpec as P

HEAD_DIM = 128
MASKED = -1e30
STEP_HEADS = 4
NT = (((1,), (1,)), ((), ()))
NN = (((1,), (0,)), ((), ()))
TN = (((0,), (0,)), ((), ()))


def dot(a, b, dims):
    return lax.dot_general(a, b, dims, preferred_element_type=jnp.float32)


def source_place(p, c, m):
    if m == 0:
        return p, c - 1
    source = p ^ m
    return source, c - jnp.where(source > p, 1, 0)


def stacked_heads(ref, first, group):
    return jnp.concatenate(
        [ref[:, j * HEAD_DIM : (j + 1) * HEAD_DIM] for j in range(first, first + group)], axis=0
    )


def add_terms(queries, douts, norm_row, delta_row, bias, keys, values, group):
    scaling = HEAD_DIM ** (-0.5)
    rows = bias.shape[1]
    scores = dot(keys, queries, NT) * scaling
    shift = jnp.concatenate([bias] * group, axis=1) - norm_row
    weights = jnp.exp(scores + shift)
    prob_grad = dot(values, douts, NT)
    grad_value = dot(weights.astype(jnp.bfloat16), douts, NN)
    score_grad = (weights * (prob_grad - delta_row)).astype(jnp.bfloat16)
    grad_key = dot(score_grad, queries, NN) * scaling
    grad_query_t = dot(keys, score_grad, TN) * scaling
    grad_query = jnp.concatenate(
        [grad_query_t[:, j * rows : (j + 1) * rows].T for j in range(group)], axis=1
    )
    return grad_query, grad_key, grad_value


def own_kernel(
    group, head_count, q_ref, do_ref, o_ref, norm_ref, ids_ref, k_ref, v_ref,
    dq_ref, dkv_ref, norm_out, delta_out, start_out, bias_ref, norm_t,
):
    g = pl.program_id(0)
    rows = q_ref.shape[0]
    blocks = ids_ref.shape[0]

    @pl.when(g == 0)
    def _():
        me = lax.axis_index("ctx") * head_count + lax.axis_index("head")
        mine = ids_ref[pl.ds(me, 1), :]
        before = jnp.zeros((1, rows), jnp.int32)
        for back in range(min(head_count, blocks - 1) + 1):
            other = jnp.maximum(me - back, 0)
            ids = jnp.broadcast_to(ids_ref[pl.ds(other, 1), :], (rows, rows)).T
            less = jnp.where((ids < mine) & (me >= back), 1, 0)
            before = before + jnp.sum(less, axis=0, keepdims=True)
        first = jnp.maximum(me - head_count, 0) * rows
        start = first + before
        start_out[...] = jnp.broadcast_to(start, start_out.shape)
        key_at = lax.broadcasted_iota(jnp.int32, (rows, rows), 0)
        query_at = lax.broadcasted_iota(jnp.int32, (rows, rows), 1)
        allowed = (key_at + me * rows >= start) & (key_at <= query_at)
        bias_ref[...] = jnp.where(allowed, 0.0, MASKED)
        norm_t[...] = norm_ref[...].T

    for i in range(k_ref.shape[1] // HEAD_DIM):
        deltas = []
        norms = []
        for j in range(i * group, (i + 1) * group):
            cols = slice(j * HEAD_DIM, (j + 1) * HEAD_DIM)
            product = do_ref[:, cols].astype(jnp.float32) * o_ref[:, cols].astype(jnp.float32)
            deltas.append(jnp.sum(product.T, axis=0, keepdims=True))
            norms.append(norm_t[pl.ds(g * (group * norm_out.shape[0]) + j, 1), :])
        delta_row = jnp.concatenate(deltas, axis=1)
        norm_row = jnp.concatenate(norms, axis=1)
        delta_out[i] = delta_row
        norm_out[i] = norm_row
        at = slice(i * HEAD_DIM, (i + 1) * HEAD_DIM)
        wide = slice(i * group * HEAD_DIM, (i + 1) * group * HEAD_DIM)
        grad_query, grad_key, grad_value = add_terms(
            stacked_heads(q_ref, i * group, group), stacked_heads(do_ref, i * group, group),
            norm_row, delta_row, bias_ref[...], k_ref[:, at], v_ref[:, at], group,
        )
        dq_ref[:, wide] = grad_query
        dkv_ref[0, :, at] = grad_key
        dkv_ref[1, :, at] = grad_value


def halo_kernel(group, head_count, classes, split, *refs):
    q_ref, do_ref, norm_ref, delta_ref, start_ref, dq_in = refs[:6]
    at = 6
    kv = []
    for pair in split:
        if pair:
            kv.append((refs[at].at[0], refs[at + 1].at[0]))
            at += 2
        else:
            kv.append((refs[at].at[0], refs[at].at[1]))
            at += 1
    dq_ref = refs[at]
    outs = refs[at + 1 : at + 1 + len(classes)]
    bias_ref = refs[-1]
    g = pl.program_id(0)
    rows = q_ref.shape[0]

    @pl.when(g == 0)
    def _():
        c = lax.axis_index("ctx")
        p = lax.axis_index("head")
        key_at = lax.broadcasted_iota(jnp.int32, (rows, rows), 0)
        for i, m in enumerate(classes):
            source, plane = source_place(p, c, m)
            allowed = key_at + (plane * head_count + source) * rows >= start_ref[:1, :]
            bias_ref[i * rows : (i + 1) * rows, :] = jnp.where(allowed, 0.0, MASKED)

    for i in range(norm_ref.shape[0]):
        at = slice(i * HEAD_DIM, (i + 1) * HEAD_DIM)
        wide = slice(i * group * HEAD_DIM, (i + 1) * group * HEAD_DIM)
        grad_query, grad_key, grad_value = add_terms(
            stacked_heads(q_ref, i * group, group), stacked_heads(do_ref, i * group, group),
            norm_ref[i], delta_ref[i], bias_ref[...],
            jnp.concatenate([k[:, at] for k, _ in kv], axis=0),
            jnp.concatenate([v[:, at] for _, v in kv], axis=0),
            group,
        )
        dq_ref[:, wide] = (dq_in[:, wide] + grad_query).astype(dq_ref.dtype)
        for n, out in enumerate(outs):
            out[0, :, at] = grad_key[n * rows : (n + 1) * rows].astype(out.dtype)
            out[1, :, at] = grad_value[n * rows : (n + 1) * rows].astype(out.dtype)


def cost(blocks, rows, width):
    return pl.CostEstimate(
        flops=10 * blocks * rows * rows * width,
        bytes_accessed=8 * rows * width + blocks * rows * width,
        transcendentals=blocks * rows * rows * width // HEAD_DIM,
    )


def own_call(query, dout, out, norm, ids, key, value, head_count):
    rows, width = query.shape
    kv_heads = key.shape[1] // HEAD_DIM
    group = width // HEAD_DIM // kv_heads
    step = min(STEP_HEADS, kv_heads)
    wide = pl.BlockSpec((rows, step * group * HEAD_DIM), lambda g: (0, g))
    thin = pl.BlockSpec((rows, step * HEAD_DIM), lambda g: (0, g))
    whole = lambda a: pl.BlockSpec(a.shape, lambda g: (0,) * a.ndim)
    row = pl.BlockSpec((step, 1, group * rows), lambda g: (g, 0, 0))
    row_shape = jax.ShapeDtypeStruct((kv_heads, 1, group * rows), jnp.float32)
    return pl.pallas_call(
        functools.partial(own_kernel, group, head_count),
        grid=(kv_heads // step,),
        in_specs=[wide, wide, wide, whole(norm), whole(ids), thin, thin],
        out_specs=[
            wide,
            pl.BlockSpec((2, rows, step * HEAD_DIM), lambda g: (0, 0, g)),
            row,
            row,
            pl.BlockSpec((8, rows), lambda g: (0, 0)),
        ],
        out_shape=[
            jax.ShapeDtypeStruct((rows, width), jnp.float32),
            jax.ShapeDtypeStruct((2,) + key.shape, jnp.float32),
            row_shape,
            row_shape,
            jax.ShapeDtypeStruct((8, rows), jnp.int32),
        ],
        scratch_shapes=[
            pltpu.VMEM((rows, rows), jnp.float32),
            pltpu.VMEM((norm.shape[1], rows), jnp.float32),
        ],
        cost_estimate=cost(1, rows, width),
        name="own_block",
    )(query, dout, out, norm, ids, key, value)


def halo_call(query, dout, norms, deltas, starts, dq, classes, held, last, head_count):
    rows, width = query.shape
    kv_heads = norms.shape[0]
    group = width // HEAD_DIM // kv_heads
    step = min(STEP_HEADS, kv_heads)
    wide = pl.BlockSpec((rows, step * group * HEAD_DIM), lambda g: (0, g))
    row = pl.BlockSpec((step, 1, group * rows), lambda g: (g, 0, 0))
    pair = pl.BlockSpec((2, rows, step * HEAD_DIM), lambda g: (0, 0, g))
    single = pl.BlockSpec((1, rows, step * HEAD_DIM), lambda g: (0, 0, g))
    flat, specs, split = [], [], []
    for item in held:
        split.append(isinstance(item, tuple))
        for part in item if isinstance(item, tuple) else (item,):
            flat.append(part)
            specs.append(single if split[-1] else pair)
    out = jax.ShapeDtypeStruct((2, rows, kv_heads * HEAD_DIM), jnp.bfloat16)
    return pl.pallas_call(
        functools.partial(halo_kernel, group, head_count, tuple(classes), tuple(split)),
        grid=(kv_heads // step,),
        in_specs=[wide, wide, row, row, pl.BlockSpec((8, rows), lambda g: (0, 0)), wide] + specs,
        out_specs=[wide] + [pair] * len(classes),
        out_shape=[jax.ShapeDtypeStruct((rows, width), jnp.bfloat16 if last else jnp.float32)]
        + [out] * len(classes),
        scratch_shapes=[pltpu.VMEM((len(classes) * rows, rows), jnp.float32)],
        cost_estimate=cost(len(classes), rows, width),
        name="halo_blocks",
    )(query, dout, norms, deltas, starts, dq, *flat)


def solution(mesh):
    head_count = mesh.shape["head"]
    ctx_count = mesh.shape["ctx"]
    names = tuple(mesh.axis_names)

    def linear(c, p):
        at = {"head": p, "ctx": c}
        index = 0
        for name in names:
            index = index * mesh.shape[name] + at[name]
        return index

    places = [(c, p) for c in range(ctx_count) for p in range(head_count)]

    def later(c, p, m):
        if m == 0:
            return c + 1, p
        return c + (1 if (p ^ m) < p else 0), p ^ m

    def permute(value, moves):
        pairs = [(linear(*a), linear(*b)) for a, b in moves]
        return lax.ppermute(value, names, pairs)

    def inside(moves):
        return [(a, b) for a, b in moves if b[0] < ctx_count]

    def wrapped(place):
        return place[0] % ctx_count, place[1]

    def send(value, m):
        moves = [((c, p), later(c, p, m)) for c, p in places]
        moves = [(a, wrapped(b)) for a, b in moves] if m else inside(moves)
        return permute(value, moves)

    def send_back(value, m):
        moves = inside([((c, p), later(c, p, m)) for c, p in places])
        return permute(value, [(b, a) for a, b in moves])

    def relay(value, m, hop):
        moves = inside([(later(c, p, m ^ hop), later(c, p, m)) for c, p in places])
        return permute(value, [(wrapped(a), b) for a, b in moves])

    def local(query, key, value, out, dout, norm, doc_ids):
        rows = query.shape[0]
        kv = jnp.stack((key, value))
        singles = [m for m in range(1, head_count) if m & (m - 1) == 0]
        held = {m: send(kv, m) for m in singles + [0]}
        levels = [singles + [0]]
        for bits in range(2, head_count.bit_length()):
            level = [m for m in range(1, head_count) if bin(m).count("1") == bits]
            for m in level:
                low, high = m & -m, 1 << (m.bit_length() - 1)
                parts = []
                for side, hop in ((0, low), (1, high)):
                    via = held[m ^ hop]
                    part = via[side] if isinstance(via, tuple) else via[side : side + 1]
                    parts.append(relay(part, m, hop))
                held[m] = tuple(parts)
            levels.append(level)
        dq, own, norms, deltas, starts = own_call(
            query, dout, out, norm, doc_ids.reshape(-1, rows), key, value, head_count
        )
        back = []
        for i, level in enumerate(levels):
            dq, *terms = halo_call(
                query, dout, norms, deltas, starts, dq, level, [held[m] for m in level],
                i == len(levels) - 1, head_count,
            )
            back += [send_back(term, m) for term, m in zip(terms, level)]
        total = own
        for term in back:
            total = total + term.astype(jnp.float32)
        total = total.astype(jnp.bfloat16)
        return dq, total[0], total[1]

    spec = P(("ctx", "head"), None)
    return jax.shard_map(
        local,
        mesh=mesh,
        in_specs=(spec,) * 6 + (P(),),
        out_specs=(spec,) * 3,
        check_vma=False,
    )
```

```python
import functools

import jax
import jax.numpy as jnp
from jax import lax
from jax.experimental import pallas as pl
from jax.experimental.pallas import tpu as pltpu
from jax.sharding import PartitionSpec as P


HEAD_DIM = 128
MASKED = -1e30
VMEM_LIMIT = 24 << 20
STEP_HEADS = 4
NT = (((1,), (1,)), ((), ()))
NN = (((1,), (0,)), ((), ()))
TN = (((0,), (0,)), ((), ()))


def dot(a, b, dims):
    return lax.dot_general(a, b, dims, preferred_element_type=jnp.float32)


def source_place(p, c, m):
    if m == 0:
        return p, c - 1
    source = p ^ m
    return source, c - jnp.where(source > p, 1, 0)


def stacked_heads(ref, first, group):
    return jnp.concatenate(
        [ref[:, j * HEAD_DIM : (j + 1) * HEAD_DIM] for j in range(first, first + group)], axis=0
    )


def add_terms(queries, douts, norm_row, delta_row, bias, keys, values, group):
    scaling = HEAD_DIM ** (-0.5)
    rows = bias.shape[1]
    scores = dot(keys, queries, NT) * scaling
    shift = jnp.concatenate([bias] * group, axis=1) - norm_row
    weights = jnp.exp(scores + shift)
    prob_grad = dot(values, douts, NT)
    grad_value = dot(weights.astype(jnp.bfloat16), douts, NN)
    score_grad = (weights * (prob_grad - delta_row)).astype(jnp.bfloat16)
    grad_key = dot(score_grad, queries, NN) * scaling
    grad_query_t = dot(keys, score_grad, TN) * scaling
    grad_query = jnp.concatenate(
        [grad_query_t[:, j * rows : (j + 1) * rows].T for j in range(group)], axis=1
    )
    return grad_query, grad_key, grad_value


def own_kernel(
    group, head_count, q_ref, do_ref, o_ref, norm_ref, ids_ref, k_ref, v_ref,
    dq_ref, dkv_ref, norm_out, delta_out, start_out, bias_ref, norm_t,
):
    g = pl.program_id(0)
    rows = q_ref.shape[0]
    blocks = ids_ref.shape[0]

    @pl.when(g == 0)
    def _():
        me = lax.axis_index("ctx") * head_count + lax.axis_index("head")
        mine = ids_ref[pl.ds(me, 1), :]
        before = jnp.zeros((1, rows), jnp.int32)
        for back in range(min(head_count, blocks - 1) + 1):
            other = jnp.maximum(me - back, 0)
            ids = jnp.broadcast_to(ids_ref[pl.ds(other, 1), :], (rows, rows)).T
            less = jnp.where((ids < mine) & (me >= back), 1, 0)
            before = before + jnp.sum(less, axis=0, keepdims=True)
        first = jnp.maximum(me - head_count, 0) * rows
        start = first + before
        start_out[...] = jnp.broadcast_to(start, start_out.shape)
        key_at = lax.broadcasted_iota(jnp.int32, (rows, rows), 0)
        query_at = lax.broadcasted_iota(jnp.int32, (rows, rows), 1)
        allowed = (key_at + me * rows >= start) & (key_at <= query_at)
        bias_ref[...] = jnp.where(allowed, 0.0, MASKED)
        norm_t[...] = norm_ref[...].T

    for i in range(k_ref.shape[1] // HEAD_DIM):
        deltas = []
        norms = []
        for j in range(i * group, (i + 1) * group):
            cols = slice(j * HEAD_DIM, (j + 1) * HEAD_DIM)
            product = do_ref[:, cols].astype(jnp.float32) * o_ref[:, cols].astype(jnp.float32)
            deltas.append(jnp.sum(product.T, axis=0, keepdims=True))
            norms.append(norm_t[pl.ds(g * (group * norm_out.shape[0]) + j, 1), :])
        delta_row = jnp.concatenate(deltas, axis=1)
        norm_row = jnp.concatenate(norms, axis=1)
        delta_out[i] = delta_row
        norm_out[i] = norm_row
        at = slice(i * HEAD_DIM, (i + 1) * HEAD_DIM)
        wide = slice(i * group * HEAD_DIM, (i + 1) * group * HEAD_DIM)
        grad_query, grad_key, grad_value = add_terms(
            stacked_heads(q_ref, i * group, group), stacked_heads(do_ref, i * group, group),
            norm_row, delta_row, bias_ref[...], k_ref[:, at], v_ref[:, at], group,
        )
        dq_ref[:, wide] = grad_query
        dkv_ref[0, :, at] = grad_key
        dkv_ref[1, :, at] = grad_value


def halo_kernel(group, head_count, classes, split, *refs):
    q_ref, do_ref, norm_ref, delta_ref, start_ref, dq_in = refs[:6]
    at = 6
    kv = []
    for pair in split:
        if pair:
            kv.append((refs[at].at[0], refs[at + 1].at[0]))
            at += 2
        else:
            kv.append((refs[at].at[0], refs[at].at[1]))
            at += 1
    dq_ref = refs[at]
    outs = refs[at + 1 : at + 1 + len(classes)]
    bias_ref = refs[-1]
    g = pl.program_id(0)
    rows = q_ref.shape[0]

    @pl.when(g == 0)
    def _():
        c = lax.axis_index("ctx")
        p = lax.axis_index("head")
        key_at = lax.broadcasted_iota(jnp.int32, (rows, rows), 0)
        for i, m in enumerate(classes):
            source, plane = source_place(p, c, m)
            allowed = key_at + (plane * head_count + source) * rows >= start_ref[:1, :]
            bias_ref[i * rows : (i + 1) * rows, :] = jnp.where(allowed, 0.0, MASKED)

    for i in range(norm_ref.shape[0]):
        at = slice(i * HEAD_DIM, (i + 1) * HEAD_DIM)
        wide = slice(i * group * HEAD_DIM, (i + 1) * group * HEAD_DIM)
        grad_query, grad_key, grad_value = add_terms(
            stacked_heads(q_ref, i * group, group), stacked_heads(do_ref, i * group, group),
            norm_ref[i], delta_ref[i], bias_ref[...],
            jnp.concatenate([k[:, at] for k, _ in kv], axis=0),
            jnp.concatenate([v[:, at] for _, v in kv], axis=0),
            group,
        )
        dq_ref[:, wide] = (dq_in[:, wide] + grad_query).astype(dq_ref.dtype)
        for n, out in enumerate(outs):
            out[0, :, at] = grad_key[n * rows : (n + 1) * rows].astype(out.dtype)
            out[1, :, at] = grad_value[n * rows : (n + 1) * rows].astype(out.dtype)


def cost(blocks, rows, width):
    return pl.CostEstimate(
        flops=10 * blocks * rows * rows * width,
        bytes_accessed=8 * rows * width + blocks * rows * width,
        transcendentals=blocks * rows * rows * width // HEAD_DIM,
    )


def own_call(query, dout, out, norm, ids, key, value, head_count):
    rows, width = query.shape
    kv_heads = key.shape[1] // HEAD_DIM
    group = width // HEAD_DIM // kv_heads
    step = min(STEP_HEADS, kv_heads)
    wide = pl.BlockSpec((rows, step * group * HEAD_DIM), lambda g: (0, g))
    thin = pl.BlockSpec((rows, step * HEAD_DIM), lambda g: (0, g))
    whole = lambda a: pl.BlockSpec(a.shape, lambda g: (0,) * a.ndim)
    row = pl.BlockSpec((step, 1, group * rows), lambda g: (g, 0, 0))
    row_shape = jax.ShapeDtypeStruct((kv_heads, 1, group * rows), jnp.float32)
    return pl.pallas_call(
        functools.partial(own_kernel, group, head_count),
        grid=(kv_heads // step,),
        in_specs=[wide, wide, wide, whole(norm), whole(ids), thin, thin],
        out_specs=[
            wide,
            pl.BlockSpec((2, rows, step * HEAD_DIM), lambda g: (0, 0, g)),
            row,
            row,
            pl.BlockSpec((8, rows), lambda g: (0, 0)),
        ],
        out_shape=[
            jax.ShapeDtypeStruct((rows, width), jnp.float32),
            jax.ShapeDtypeStruct((2,) + key.shape, jnp.float32),
            row_shape,
            row_shape,
            jax.ShapeDtypeStruct((8, rows), jnp.int32),
        ],
        scratch_shapes=[
            pltpu.VMEM((rows, rows), jnp.float32),
            pltpu.VMEM((norm.shape[1], rows), jnp.float32),
        ],
        cost_estimate=cost(1, rows, width),
        compiler_params=pltpu.CompilerParams(vmem_limit_bytes=VMEM_LIMIT),
        name="own_block",
    )(query, dout, out, norm, ids, key, value)


def halo_call(query, dout, norms, deltas, starts, dq, classes, held, last, head_count):
    rows, width = query.shape
    kv_heads = norms.shape[0]
    group = width // HEAD_DIM // kv_heads
    step = min(STEP_HEADS, kv_heads)
    wide = pl.BlockSpec((rows, step * group * HEAD_DIM), lambda g: (0, g))
    row = pl.BlockSpec((step, 1, group * rows), lambda g: (g, 0, 0))
    pair = pl.BlockSpec((2, rows, step * HEAD_DIM), lambda g: (0, 0, g))
    single = pl.BlockSpec((1, rows, step * HEAD_DIM), lambda g: (0, 0, g))
    flat, specs, split = [], [], []
    for item in held:
        split.append(isinstance(item, tuple))
        for part in item if isinstance(item, tuple) else (item,):
            flat.append(part)
            specs.append(single if split[-1] else pair)
    out = jax.ShapeDtypeStruct((2, rows, kv_heads * HEAD_DIM), jnp.bfloat16)
    return pl.pallas_call(
        functools.partial(halo_kernel, group, head_count, tuple(classes), tuple(split)),
        grid=(kv_heads // step,),
        in_specs=[wide, wide, row, row, pl.BlockSpec((8, rows), lambda g: (0, 0)), wide] + specs,
        out_specs=[wide] + [pair] * len(classes),
        out_shape=[jax.ShapeDtypeStruct((rows, width), jnp.bfloat16 if last else jnp.float32)]
        + [out] * len(classes),
        scratch_shapes=[pltpu.VMEM((len(classes) * rows, rows), jnp.float32)],
        cost_estimate=cost(len(classes), rows, width),
        compiler_params=pltpu.CompilerParams(vmem_limit_bytes=VMEM_LIMIT),
        name="halo_blocks",
    )(query, dout, norms, deltas, starts, dq, *flat)


def solution(mesh):
    head_count = mesh.shape["head"]
    ctx_count = mesh.shape["ctx"]
    names = tuple(mesh.axis_names)

    def linear(c, p):
        at = {"head": p, "ctx": c}
        index = 0
        for name in names:
            index = index * mesh.shape[name] + at[name]
        return index

    places = [(c, p) for c in range(ctx_count) for p in range(head_count)]

    def later(c, p, m):
        if m == 0:
            return c + 1, p
        return c + (1 if (p ^ m) < p else 0), p ^ m

    def permute(value, moves):
        pairs = []
        for (c, p), (c2, p2) in moves:
            pairs.append((linear(c % ctx_count, p), linear(c2 % ctx_count, p2)))
        return lax.ppermute(value, names, pairs)

    def send(value, m):
        return permute(value, [((c, p), later(c, p, m)) for c, p in places])

    def send_back(value, m):
        return permute(value, [(later(c, p, m), (c, p)) for c, p in places])

    def relay(value, m, hop):
        return permute(value, [(later(c, p, m ^ hop), later(c, p, m)) for c, p in places])

    def local(query, key, value, out, dout, norm, doc_ids):
        rows = query.shape[0]
        kv = jnp.stack((key, value))
        singles = [m for m in range(1, head_count) if m & (m - 1) == 0]
        held = {m: send(kv, m) for m in singles + [0]}
        levels = [singles + [0]]
        for bits in range(2, head_count.bit_length()):
            level = [m for m in range(1, head_count) if bin(m).count("1") == bits]
            for m in level:
                low, high = m & -m, 1 << (m.bit_length() - 1)
                parts = []
                for side, hop in ((0, low), (1, high)):
                    via = held[m ^ hop]
                    part = via[side] if isinstance(via, tuple) else via[side : side + 1]
                    parts.append(relay(part, m, hop))
                held[m] = tuple(parts)
            levels.append(level)
        dq, own, norms, deltas, starts = own_call(
            query, dout, out, norm, doc_ids.reshape(-1, rows), key, value, head_count
        )
        back = []
        for i, level in enumerate(levels):
            dq, *terms = halo_call(
                query, dout, norms, deltas, starts, dq, level, [held[m] for m in level],
                i == len(levels) - 1, head_count,
            )
            back += [send_back(term, m) for term, m in zip(terms, level)]
        total = own
        for term in back:
            total = total + term.astype(jnp.float32)
        total = total.astype(jnp.bfloat16)
        return dq, total[0], total[1]

    spec = P(("ctx", "head"), None)
    return jax.shard_map(
        local,
        mesh=mesh,
        in_specs=(spec,) * 6 + (P(),),
        out_specs=(spec,) * 3,
        check_vma=False,
    )
```
